32 devices in a mesh: dist: 4 (over y, x), rows: 8 (over z, core).
Axes of the slice: x: 2, y: 2, z: 4, core: 2. Of those that a mesh axis runs over, the one named last changes fastest.
Arguments:
- volume: bfloat16 [128, 128, 2048], P('rows', None, 'dist'), may hold values from -6 to 6
- kernels: bfloat16 [128, 2, 128, 128], P('rows'), may hold values from -0.09375 to 0.09375
- targets: int32 [128, 2], P('rows'), may hold values from 0 to 7, all different within a row; in each aligned block of 16 rows (0 to 15, 16 to 31, ...) at most 8 rows name the same one
- contrast: bfloat16 [4, 8, 128, 2048], P('dist', 'rows'), may hold values from -6 to 6
- fresnel_numbers: float32 [4], P('dist'), may hold values from 0.4 to 1.6
Outputs:
- gradient: bfloat16 [128, 128, 2048], P('rows', None, 'dist')
The draws below stay inside these ranges and needn't reach their ends.
Inputs may be any that keep to these rules, and one draw needn't show every extreme that they name: `targets`: each row names 2 different detector blocks; among the rows of one index of rows no detector block is named more than 8 times, and some block is named exactly 8 times.
All inputs are finite; a program needn't handle non-finite values.
Results may differ from the reference program's by a relative error of at most 0.0063.
Values may be sent and summed in bfloat16 or wider, within the bound.
No kernel may reach another device: no remote copies, remote signals or barrier semaphores. Data moves between devices by JAX's collectives and lax.ppermute only.
A program may use at most 128 MiB of HBM per device.

```python
import math
import jax
import jax.numpy as jnp
import numpy as np
from jax import lax

W = 2048
BLK = 128
TOP = 2
VB_DEV = 16
VBLK = 128
NDIST = 4
MOST = 8
N_ROWS = 8


def level_of(own_key, dims, cuts, smallest, largest):
    factor_of, own = 1.0, jax.random.fold_in(own_key, 6)
    for axis_at, shards_of in cuts:
        steps = jnp.exp(jax.random.uniform(jax.random.fold_in(own, axis_at), (shards_of,), jnp.float32, smallest / len(cuts), largest / len(cuts)))
        factor_of = factor_of * jnp.repeat(steps, dims[axis_at] // shards_of).reshape([-1 if axis == axis_at else 1 for axis in range(len(dims))])
    return factor_of


def deal_out(key, own, number, rows, number_of, top, bound, skew):
    sequence = jax.random.permutation(key, number_of)
    packed, usual = portions_of(number_of, rows * top, bound, skew, True), portions_of(number_of, rows * top, bound, skew, False)
    places = jnp.arange(number_of)

    def named(sizes, turn):
        used = int((sizes > 0).sum())
        fixed = max(1, used // 4)
        shifted = fixed + (places - fixed + turn * (used - fixed)) % max(1, number_of - fixed)
        return jnp.zeros((number_of,), jnp.int32).at[sequence[jnp.where(places < fixed, places, shifted)]].set(jnp.asarray(sizes, jnp.int32))

    sizes = jnp.where(number % 4 == 0, named(packed, number // 4), named(usual, number - number // 4 - 1))
    mixed = jax.random.permutation(jax.random.fold_in(own, 3), number_of)
    donor, taker = mixed[0:number_of // 2 * 2:2], mixed[1:number_of // 2 * 2:2]
    margin = jnp.minimum(sizes[donor] - 1, bound - sizes[taker]) // 2
    margin = jnp.where((donor == sequence[0]) | (taker == sequence[0]) | (sizes[taker] == 0), 0, jnp.maximum(margin, 0))
    shifted = jax.random.randint(jax.random.fold_in(own, 4), (number_of // 2,), 0, 1 << 20) % (margin + 1)
    sizes = sizes.at[donor].add(-shifted).at[taker].add(shifted)
    labels = jnp.searchsorted(jnp.cumsum(sizes), jnp.arange(rows * top), side="right").astype(jnp.int32)
    grid = labels.reshape(top, rows).T
    grid = grid[jax.random.permutation(jax.random.fold_in(own, 1), rows)]
    turn = jax.random.randint(jax.random.fold_in(own, 2), (rows, 1), 0, top)
    return jnp.take_along_axis(grid, (jnp.arange(top)[None, :] + turn) % top, axis=1)


def portions_of(number_of, total, most, skew, full):
    weights = [(1 << 20) // math.isqrt(rank ** skew) + 1 for rank in range(1, number_of + 1)]
    largest = most if full else min(most, max(-(-total // number_of), total * weights[0] // sum(weights)))
    least = 1 if total - largest >= number_of - 1 else 0
    holding, rest = [largest] + [least] * (number_of - 1), total - largest - least * (number_of - 1)
    while rest > 0:
        candidates = [i for i in range(1, number_of) if holding[i] < largest] or [i for i in range(1, number_of) if holding[i] < most]
        whole, left = sum([weights[i] for i in candidates]), rest
        for i in candidates:
            extra = min(most - holding[i], max(1, left * weights[i] // whole), rest)
            holding[i] = holding[i] + extra
            rest = rest - extra
    return np.array(holding)


def normal_values(own_key, shape, scale, limit, shards=(), held_as=jnp.bfloat16):
    result = scale * jax.random.normal(own_key, shape, jnp.float32)
    if shards:
        result = result * level_of(own_key, shape, shards, -0.22, 0.18)
    return jnp.clip(result, -limit, limit).astype(held_as)


def setup_inputs(seed: int = 0) -> dict:
    splits = jax.random.split(jax.random.key(seed), 6)
    volume = normal_values(splits[0], (VBLK, BLK, W), 1.0, 6.0, ((0, 8), (2, 4)))
    kernels = normal_values(splits[1], (VBLK, TOP, BLK, BLK), (BLK * TOP * VB_DEV) ** -0.5, 0.09375, ((0, 8),))
    targets_keys = jax.random.split(jax.random.fold_in(splits[2], 1), VBLK // VB_DEV)
    targets_turns = jax.random.permutation(jax.random.fold_in(splits[2], 3), VBLK // VB_DEV)
    targets = jax.vmap(lambda own, number: deal_out(jax.random.fold_in(splits[2], 2), own, number, VB_DEV, N_ROWS, TOP, MOST, 2))(targets_keys, targets_turns).reshape((VBLK, TOP))
    contrast = normal_values(splits[3], (NDIST, N_ROWS, BLK, W), 1.0, 6.0, ((0, 4), (1, 8)))
    fresnel_numbers = jnp.clip(jnp.exp(math.log(1.6) - 1.3862944 * jax.random.uniform(splits[4], (NDIST,), jnp.float32) ** level_of(splits[4], (NDIST,), ((0, 4),), -0.2, 0.2)), 0.4, 1.6)
    return {"volume": volume, "kernels": kernels, "targets": targets, "contrast": contrast, "fresnel_numbers": fresnel_numbers}


def fresnel_apply(field, numbers):
    freq = jnp.arange(W // 2 + 1).astype(jnp.float32)
    factor = jnp.sin(jnp.pi * numbers * freq * freq / W)
    spectrum = jnp.fft.rfft(field, axis=-1) * factor
    return jnp.fft.irfft(spectrum, n=W, axis=-1).astype(field.dtype)


def reference(volume, kernels, targets, contrast, fresnel_numbers):
    owners = N_ROWS
    items = VB_DEV * TOP
    vol = volume.reshape(owners, VB_DEV, BLK, W)
    ker = kernels.reshape(owners, VB_DEV, TOP, BLK, BLK)
    tgt = targets.reshape(owners, items)

    def send(carry, pieces):
        vpart, kpart, tpart = pieces
        contrib = jnp.einsum("btij,bjw->btiw", kpart.astype(jnp.float32), vpart.astype(jnp.float32))
        contrib = contrib.astype(jnp.bfloat16).reshape(items, BLK * W)
        onehot = (tpart[None, :] == jnp.arange(owners, dtype=jnp.int32)[:, None]).astype(jnp.float32)
        part = jnp.dot(onehot, contrib.astype(jnp.float32), precision=lax.Precision.HIGHEST,
                       preferred_element_type=jnp.float32).astype(jnp.bfloat16)
        return carry + part.astype(jnp.float32).reshape(owners, BLK, W), None

    start = jnp.zeros((owners, BLK, W), jnp.float32)
    projection, _ = lax.scan(send, start, (vol, ker, tgt))
    numbers = fresnel_numbers.reshape(NDIST, 1, 1, 1)
    residual = -2.0 * fresnel_apply(jnp.broadcast_to(projection[None], (NDIST, owners, BLK, W)), numbers)
    residual = residual - contrast.astype(jnp.float32)
    image_gradient = jnp.sum(-2.0 * fresnel_apply(residual, numbers), axis=0).astype(jnp.bfloat16)

    def back(pieces):
        kpart, tpart = pieces
        chosen = image_gradient[tpart]
        grad = jnp.einsum("btij,btiw->bjw", kpart.astype(jnp.float32), chosen.astype(jnp.float32))
        return grad.astype(jnp.bfloat16)

    grads = lax.map(back, (ker, targets.reshape(owners, VB_DEV, TOP)))
    return grads.reshape(VB_DEV * owners, BLK, W)
```

```python
import functools
import math

import jax
import jax.numpy as jnp
from jax import lax
from jax.experimental import pallas as pl
from jax.experimental.pallas import tpu as pltpu
from jax.sharding import PartitionSpec as P

BF16 = jnp.bfloat16
F32 = jnp.float32
DEEP = 256


def whole(memory_space=pltpu.VMEM):
    return pl.BlockSpec(memory_space=memory_space)


def swap(x, axis, mask):
    size = lax.axis_size(axis)
    return lax.ppermute(x, axis, [(i, i ^ mask) for i in range(size)])


def cost(flops, nbytes):
    return pl.CostEstimate(flops=flops, bytes_accessed=nbytes, transcendentals=0)


def project_kernel(me_ref, targets_ref, kernels_ref, volume_ref, send_ref, keep_ref, acc):
    step = pl.program_id(0)
    group, blk, _ = volume_ref.shape
    top = kernels_ref.shape[1]
    half = send_ref.shape[0]

    @pl.when(step == 0)
    def _():
        acc[...] = jnp.zeros_like(acc)

    me = me_ref[0]
    for b in range(group):
        product = jnp.dot(
            kernels_ref[b].reshape(top * blk, blk), volume_ref[b], preferred_element_type=F32
        )
        product = product.astype(BF16).astype(F32)
        for t in range(top):
            rel = targets_ref[step * group + b, t] ^ me
            slot = (rel & 1) * half + (rel >> 1)
            acc[slot] += product[t * blk : (t + 1) * blk]

    @pl.when(step == pl.num_programs(0) - 1)
    def _():
        keep_ref[...] = acc[:half].astype(BF16)
        send_ref[...] = acc[half:].astype(BF16)


def project(me, targets, kernels, volume, owners):
    vblocks, blk, quarter = volume.shape
    top = kernels.shape[1]
    half = owners // 2
    group = 4
    out = jax.ShapeDtypeStruct((half, blk, quarter), BF16)
    return pl.pallas_call(
        project_kernel,
        out_shape=(out, out),
        grid_spec=pltpu.PrefetchScalarGridSpec(
            num_scalar_prefetch=2,
            grid=(vblocks // group,),
            in_specs=[
                pl.BlockSpec((group, top, blk, blk), lambda s, *_: (s, 0, 0, 0)),
                pl.BlockSpec((group, blk, quarter), lambda s, *_: (s, 0, 0)),
            ],
            out_specs=[
                pl.BlockSpec((half, blk, quarter), lambda s, *_: (0, 0, 0)),
                pl.BlockSpec((half, blk, quarter), lambda s, *_: (0, 0, 0)),
            ],
            scratch_shapes=[pltpu.VMEM((owners, blk, quarter), F32)],
        ),
        cost_estimate=cost(2 * vblocks * top * blk * blk * quarter, 4 * 2**20),
        name="project",
    )(me, targets, kernels, volume)


def pair_kernel(keep_ref, came_ref, own_ref, *out_refs):
    own_ref[...] = keep_ref[0].astype(F32) + came_ref[0].astype(F32)
    for k, ref in enumerate(out_refs):
        ref[...] = (keep_ref[k + 1].astype(F32) + came_ref[k + 1].astype(F32)).astype(BF16)


def pair_sum(keep, came):
    half, blk, quarter = keep.shape
    return pl.pallas_call(
        pair_kernel,
        out_shape=[jax.ShapeDtypeStruct((blk, quarter), F32)]
        + [jax.ShapeDtypeStruct((blk, quarter), BF16)] * (half - 1),
        in_specs=[whole()] * 2,
        out_specs=[whole()] * half,
        cost_estimate=cost(half * blk * quarter, 6 * half * blk * quarter),
        name="pair_sum",
    )(keep, came)


def total_kernel(own_ref, *refs):
    total_ref, rounded_ref = refs[-2:]
    total = own_ref[...]
    for ref in refs[:-2]:
        total += ref[...].astype(F32)
    total_ref[...] = total
    rounded_ref[...] = total.astype(BF16)


def total_sum(own, came):
    return pl.pallas_call(
        total_kernel,
        out_shape=(
            jax.ShapeDtypeStruct(own.shape, F32),
            jax.ShapeDtypeStruct(own.shape, BF16),
        ),
        in_specs=[whole()] * (1 + len(came)),
        out_specs=[whole()] * 2,
        cost_estimate=cost(own.size * len(came), 8 * own.size),
        name="total_sum",
    )(own, *came)


def spectra(numbers, own, width, long):
    short = width // long
    k1 = lax.broadcasted_iota(jnp.int32, (short, long), 0)
    k2 = lax.broadcasted_iota(jnp.int32, (short, long), 1)
    freq = k1 + short * k2
    freq = jnp.minimum(freq, width - freq).astype(F32)
    squares = jnp.zeros((short, long), F32)
    for number in numbers:
        factor = jnp.sin(jnp.pi * number * freq * freq / width)
        squares += factor * factor
    both = 4.0 * squares - 4.0 * len(numbers) / 2
    single = 2.0 * jnp.sin(jnp.pi * own * freq * freq / width)
    return jnp.concatenate([both, single], axis=0)


def table_kernel(width, spectra_ref, contrast_ref, me_ref, table_ref, *refs):
    u_refs, extended = refs[:-1], refs[-1]
    rows2, long = spectra_ref.shape
    short = rows2 // 2
    n_dist = len(u_refs)
    quarter = width // n_dist

    def turns(shape, period, scale=1):
        a = lax.broadcasted_iota(jnp.int32, shape, 0)
        b = lax.broadcasted_iota(jnp.int32, shape, 1)
        angle = (a * b % period).astype(F32) * (2.0 * math.pi / period)
        return jnp.cos(angle), jnp.sin(angle)

    def mm(a, b):
        return jnp.dot(a, b, precision=lax.Precision.HIGHEST, preferred_element_type=F32)

    long_c, long_s = turns((long, long), long)
    twist_c, twist_s = turns((short, long), width)
    short_c, short_s = turns((short, short), short)
    spec = spectra_ref[...]
    yc, ys = mm(spec, long_c), mm(spec, long_s)
    for which in range(2):
        rows = slice(which * short, (which + 1) * short)
        re = yc[rows] * twist_c - ys[rows] * twist_s
        im = yc[rows] * twist_s + ys[rows] * twist_c
        g = (mm(short_c, re) - mm(short_s, im)) * (1.0 / width)
        line = jnp.concatenate([g[i : i + 1] for i in range(short)], axis=1)
        spread = jnp.broadcast_to(line, (DEEP, width))
        matrix = pltpu.roll(spread, 0, 1, stride=1, stride_axis=0).astype(BF16)
        if which == 0:
            table_ref[:, :width] = matrix
            table_ref[:, width:] = matrix[:, :quarter]
        else:
            extended[:, :width] = matrix
            extended[:, width:] = matrix
    me = me_ref[0]
    for k, ref in enumerate(u_refs):
        at = (me ^ k) * quarter
        total = jnp.zeros(ref.shape, F32)
        for i in range(width // DEEP):
            start = pl.multiple_of(width - i * DEEP + at, 128)
            start = pl.multiple_of(lax.rem(start, width), 128)
            total += jnp.dot(
                contrast_ref[:, i * DEEP : (i + 1) * DEEP],
                extended[:, pl.ds(start, quarter)],
                preferred_element_type=F32,
            )
        ref[...] = total.astype(BF16)


def tables(spectrum, contrast, me, n_dist):
    blk, width = contrast.shape
    quarter = width // n_dist
    return pl.pallas_call(
        functools.partial(table_kernel, width),
        out_shape=[jax.ShapeDtypeStruct((DEEP, width + quarter), BF16)]
        + [jax.ShapeDtypeStruct((blk, quarter), BF16)] * n_dist,
        in_specs=[whole(), whole(), whole(pltpu.SMEM)],
        out_specs=[whole()] * (1 + n_dist),
        scratch_shapes=[pltpu.VMEM((DEEP, 2 * width), BF16)],
        cost_estimate=cost(2 * blk * width * width, 3 * 2**20),
        name="tables",
    )(spectrum, contrast, me)


def filter_kernel(n_dist, me_ref, own_ref, table_ref, *refs):
    parts, terms, out_ref = refs[:n_dist], refs[n_dist:-1], refs[-1]
    blk, quarter = own_ref.shape
    width = n_dist * quarter
    me = me_ref[0]
    total = (2.0 * n_dist) * own_ref[...]
    for ref in terms:
        total += ref[...].astype(F32)
    for k, ref in enumerate(parts):
        for h in range(quarter // DEEP):
            start = (me - (me ^ k)) * quarter - h * DEEP + width
            start = pl.multiple_of(lax.rem(start, width), 128)
            total += jnp.dot(
                ref[:, h * DEEP : (h + 1) * DEEP],
                table_ref[:, pl.ds(start, quarter)],
                preferred_element_type=F32,
            )
    out_ref[...] = total.astype(BF16)


def filtered(me, own, table, parts, terms):
    blk, quarter = own.shape
    n_dist = len(parts)
    return pl.pallas_call(
        functools.partial(filter_kernel, n_dist),
        out_shape=jax.ShapeDtypeStruct((blk, quarter), BF16),
        in_specs=[whole(pltpu.SMEM)] + [whole()] * (2 + len(parts) + len(terms)),
        out_specs=whole(),
        cost_estimate=cost(2 * blk * quarter * quarter * n_dist, 3 * 2**20),
        name="filter",
    )(me, own, table, *parts, *terms)


def back_kernel(owners, me_ref, targets_ref, kernels_ref, *refs):
    parts, out_ref, chosen = refs[:owners], refs[owners], refs[owners + 1]
    step = pl.program_id(0)
    group, blk, quarter = out_ref.shape
    top = kernels_ref.shape[1]

    @pl.when(step == 0)
    def _():
        for k, ref in enumerate(parts):
            chosen[k] = ref[...]

    me = me_ref[0]
    for b in range(group):
        picked = [chosen[targets_ref[step * group + b, t] ^ me] for t in range(top)]
        out_ref[b] = lax.dot_general(
            kernels_ref[b].reshape(top * blk, blk),
            jnp.concatenate(picked, axis=0),
            (((0,), (0,)), ((), ())),
            preferred_element_type=F32,
        ).astype(BF16)


def back(me, targets, kernels, parts):
    vblocks, top, blk, _ = kernels.shape
    owners = len(parts)
    quarter = parts[0].shape[1]
    group = 4
    return pl.pallas_call(
        functools.partial(back_kernel, owners),
        out_shape=jax.ShapeDtypeStruct((vblocks, blk, quarter), BF16),
        grid_spec=pltpu.PrefetchScalarGridSpec(
            num_scalar_prefetch=2,
            grid=(vblocks // group,),
            in_specs=[pl.BlockSpec((group, top, blk, blk), lambda s, *_: (s, 0, 0, 0))]
            + [pl.BlockSpec((blk, quarter), lambda s, *_: (0, 0))] * owners,
            out_specs=pl.BlockSpec((group, blk, quarter), lambda s, *_: (s, 0, 0)),
            scratch_shapes=[pltpu.VMEM((owners, blk, quarter), BF16)],
        ),
        cost_estimate=cost(2 * vblocks * top * blk * blk * quarter, 4 * 2**20),
        name="back",
    )(me, targets, kernels, *parts)


def shards(volume, kernels, targets, contrast, fresnel_numbers):
    owners, n_dist = lax.axis_size("rows"), lax.axis_size("dist")
    me_rows = lax.axis_index("rows").astype(jnp.int32).reshape(1)
    me_dist = lax.axis_index("dist").astype(jnp.int32).reshape(1)
    half = owners // 2
    width = contrast.shape[-1]

    send, keep = project(me_rows, targets, kernels, volume, owners)
    came = swap(send, "rows", 1)
    own, *outgoing = pair_sum(keep, came)
    arrived = [swap(x, "rows", 2 * (k + 1)) for k, x in enumerate(outgoing)]

    numbers = [fresnel_numbers] + [swap(fresnel_numbers, "dist", k) for k in range(1, n_dist)]
    spectrum = spectra([x[0] for x in numbers], fresnel_numbers[0], width, 128)
    table, *terms = tables(spectrum, contrast[0, 0], me_dist, n_dist)
    terms = [terms[0]] + [swap(terms[k], "dist", k) for k in range(1, n_dist)]

    total, rounded = total_sum(own, arrived)
    parts = [rounded] + [swap(rounded, "dist", k) for k in range(1, n_dist)]
    image = filtered(me_dist, total, table, parts, terms)

    pieces = []
    for k in range(half):
        piece = image if k == 0 else swap(image, "rows", 2 * k)
        pieces += [piece, swap(piece, "rows", 1)]
    return back(me_rows, targets, kernels, pieces)


def solution(mesh):
    in_specs = (
        P("rows", None, "dist"),
        P("rows", None, None, None),
        P("rows", None),
        P("dist", "rows", None, None),
        P("dist"),
    )
    out_specs = P("rows", None, "dist")
    return jax.shard_map(shards, mesh=mesh, in_specs=in_specs, out_specs=out_specs, check_vma=False)
```

```python
import functools
import math

import jax
import jax.numpy as jnp
from jax import lax
from jax.experimental import pallas as pl
from jax.experimental.pallas import tpu as pltpu
from jax.sharding import PartitionSpec as P


BF16 = jnp.bfloat16
F32 = jnp.float32
DEEP = 256
SPLIT = (1, 1)
MIB = 2**20


def whole(memory_space=pltpu.VMEM):
    return pl.BlockSpec(memory_space=memory_space)


def swap(x, axis, mask):
    size = lax.axis_size(axis)
    return lax.ppermute(x, axis, [(i, i ^ mask) for i in range(size)])


def chunks_of(blk):
    unit = blk // sum(SPLIT)
    starts = [unit * sum(SPLIT[:i]) for i in range(len(SPLIT))]
    return [(start, unit * size) for start, size in zip(starts, SPLIT)]


def cost(flops, nbytes):
    return pl.CostEstimate(flops=flops, bytes_accessed=nbytes, transcendentals=0)


def room(nbytes):
    return pltpu.CompilerParams(vmem_limit_bytes=int(nbytes) + 4 * MIB)


def project_kernel(me_ref, *refs):
    targets_hbm, kernels_hbm, volume_hbm, send_ref, keep_ref = refs[:5]
    targets, kernels, volume, acc, sems, target_sem = refs[5:]
    vblocks, top, blk, _ = kernels.shape
    half = send_ref.shape[0]

    group = 4
    steps = vblocks // group

    def copies(step):
        part = pl.ds(step * group, group)
        return (
            pltpu.make_async_copy(volume_hbm.at[part], volume.at[part], sems.at[0, step]),
            pltpu.make_async_copy(kernels_hbm.at[part], kernels.at[part], sems.at[1, step]),
        )

    get_targets = pltpu.make_async_copy(targets_hbm, targets, target_sem)
    get_targets.start()
    for step in range(steps):
        for copy in copies(step):
            copy.start()
    acc[...] = jnp.zeros_like(acc)
    get_targets.wait()
    me = me_ref[0]

    def body(step, carry):
        for copy in copies(step):
            copy.wait()
        for i in range(group):
            b = step * group + i
            product = jnp.dot(
                kernels[b].reshape(top * blk, blk), volume[b], preferred_element_type=F32
            )
            for t in range(top):
                rel = targets[t, b] ^ me
                slot = (rel & 1) * half + (rel >> 1)
                acc[slot] += product[t * blk : (t + 1) * blk]
        return carry

    lax.fori_loop(0, steps, body, 0)
    send_ref[...] = acc[half:].astype(BF16)
    keep_ref[...] = acc[:half].astype(BF16)


def project(me, targets, kernels, volume, owners):
    vblocks, blk, quarter = volume.shape
    top = kernels.shape[1]
    half = owners // 2
    out = jax.ShapeDtypeStruct((half, blk, quarter), BF16)
    return pl.pallas_call(
        project_kernel,
        out_shape=(out, out),
        in_specs=[whole(pltpu.SMEM)] + [whole(pltpu.HBM)] * 3,
        out_specs=[whole()] * 2,
        scratch_shapes=[
            pltpu.SMEM(targets.shape, jnp.int32),
            pltpu.VMEM(kernels.shape, BF16),
            pltpu.VMEM(volume.shape, BF16),
            pltpu.VMEM((owners, blk, quarter), F32),
            pltpu.SemaphoreType.DMA((2, vblocks)),
            pltpu.SemaphoreType.DMA,
        ],
        compiler_params=room(8 * owners * blk * quarter + 8 * MIB),
        cost_estimate=cost(2 * vblocks * top * blk * blk * quarter, 4 * MIB),
        name="project",
    )(me, *(pltpu.with_memory_space_constraint(x, pltpu.HBM) for x in (targets, kernels, volume)))


def pair_kernel(chunks, keep_ref, came_ref, *out_refs):
    half, blk, _ = keep_ref.shape
    rows = blk // chunks
    for i, ref in enumerate(out_refs):
        c, k = divmod(i, half)
        part = slice(c * rows, (c + 1) * rows)
        total = keep_ref[k, part].astype(F32) + came_ref[k, part].astype(F32)
        ref[...] = total.astype(ref.dtype)


def pair_sum(keep, came, chunks):
    half, blk, quarter = keep.shape
    rows = blk // chunks
    outs = [jax.ShapeDtypeStruct((rows, quarter), BF16 if k else F32) for k in range(half)]
    return pl.pallas_call(
        functools.partial(pair_kernel, chunks),
        out_shape=outs * chunks,
        in_specs=[whole()] * 2,
        out_specs=[whole()] * (half * chunks),
        compiler_params=room(8 * half * blk * quarter),
        cost_estimate=cost(half * blk * quarter, 6 * half * blk * quarter),
        name="pair_sum",
    )(keep, came)


def total_kernel(own_ref, *refs):
    n = len(SPLIT)
    came, total_refs, rounded_refs = refs[: -2 * n], refs[-2 * n : -n], refs[-n:]
    for c, (start, rows) in enumerate(chunks_of(own_ref.shape[0])):
        part = slice(start, start + rows)
        total = own_ref[part]
        for ref in came:
            total += ref[part].astype(F32)
        total_refs[c][...] = total
        rounded_refs[c][...] = total.astype(BF16)


def total_sum(own, came):
    blk, quarter = own.shape
    shapes = [(rows, quarter) for _, rows in chunks_of(blk)]
    outs = pl.pallas_call(
        total_kernel,
        out_shape=[jax.ShapeDtypeStruct(shape, d) for d in (F32, BF16) for shape in shapes],
        in_specs=[whole()] * (1 + len(came)),
        out_specs=[whole()] * (2 * len(shapes)),
        compiler_params=room((10 + 2 * len(came)) * own.size),
        cost_estimate=cost(own.size * len(came), 8 * own.size),
        name="total_sum",
    )(own, *came)
    return outs[: len(shapes)], outs[len(shapes) :]


def mm(a, b):
    return jnp.dot(a, b, precision=lax.Precision.HIGHEST, preferred_element_type=F32)


def turns(shape, period):
    a = lax.broadcasted_iota(jnp.int32, shape, 0)
    b = lax.broadcasted_iota(jnp.int32, shape, 1)
    angle = (a * b % period).astype(F32) * (2.0 * math.pi / period)
    return jnp.cos(angle), jnp.sin(angle)


def frequencies(short, long):
    k1 = lax.broadcasted_iota(jnp.int32, (short, long), 0)
    k2 = lax.broadcasted_iota(jnp.int32, (short, long), 1)
    freq = k1 + short * k2
    return jnp.minimum(freq, short * long - freq).astype(F32)


def circulant(spec):
    short, long = spec.shape
    width = short * long
    long_c, long_s = turns((long, long), long)
    twist_c, twist_s = turns((short, long), width)
    short_c, short_s = turns((short, short), short)
    yc, ys = mm(spec, long_c), mm(spec, long_s)
    re = yc * twist_c - ys * twist_s
    im = yc * twist_s + ys * twist_c
    g = (mm(short_c, re) - mm(short_s, im)) * (1.0 / width)
    line = jnp.concatenate([g[i : i + 1] for i in range(short)], axis=1)
    spread = jnp.broadcast_to(line, (DEEP, width))
    return pltpu.roll(spread, 0, 1, stride=1, stride_axis=0).astype(BF16)


def circ_kernel(number_ref, table_ref):
    width = table_ref.shape[1] // 2
    short, long = width // 128, 128
    freq = frequencies(short, long)
    number = jnp.full((short, long), number_ref[0], F32)
    matrix = circulant(2.0 * jnp.sin(jnp.pi * number * freq * freq / width))
    table_ref[:, :width] = matrix
    table_ref[:, width:] = matrix


def circ(number, width):
    return pl.pallas_call(
        circ_kernel,
        out_shape=jax.ShapeDtypeStruct((DEEP, 2 * width), BF16),
        in_specs=[whole(pltpu.SMEM)],
        out_specs=whole(),
        compiler_params=room(8 * MIB),
        cost_estimate=cost(2**24, 3 * MIB),
        name="circ",
    )(number)


def term_kernel(number_ref, me_ref, contrast_ref, table_ref, *out_refs):
    n_dist = len(out_refs)
    blk, width = contrast_ref.shape
    quarter = width // n_dist
    me = me_ref[0]
    value = jnp.full((16, quarter), number_ref[0], F32)
    for k, ref in enumerate(out_refs):
        at = (me ^ k) * quarter
        total = jnp.zeros((blk, quarter), F32)
        for i in range(width // DEEP):
            start = pl.multiple_of(lax.rem(width - i * DEEP + at, width), 128)
            total += jnp.dot(
                contrast_ref[:, i * DEEP : (i + 1) * DEEP],
                table_ref[:, pl.ds(start, quarter)],
                preferred_element_type=F32,
            )
        ref[:blk] = total.astype(BF16)
        if k:
            rest, parts = value, []
            for _ in range(3):
                parts.append(rest.astype(BF16).astype(F32))
                rest = rest - parts[-1]
            which = lax.broadcasted_iota(jnp.int32, value.shape, 0)
            packed = jnp.where(which == 0, parts[0], jnp.where(which == 1, parts[1], parts[2]))
            ref[blk:] = packed.astype(BF16)


def terms_of(number, me, contrast, table, n_dist):
    blk, width = contrast.shape
    quarter = width // n_dist
    return pl.pallas_call(
        term_kernel,
        out_shape=[
            jax.ShapeDtypeStruct((blk + (16 if k else 0), quarter), BF16) for k in range(n_dist)
        ],
        in_specs=[whole(pltpu.SMEM), whole(pltpu.SMEM), whole(), whole()],
        out_specs=[whole()] * n_dist,
        compiler_params=room(12 * MIB),
        cost_estimate=cost(2 * blk * width * width, 3 * MIB),
        name="terms",
    )(number, me, contrast, table)


def table_kernel(number_ref, *refs):
    term_refs, (table_ref, sum_ref) = refs[:-2], refs[-2:]
    blk, quarter = sum_ref.shape
    width = table_ref.shape[1] - quarter
    short, long = width // 128, 128
    freq = frequencies(short, long)
    total = term_refs[0][...].astype(F32)
    factor = jnp.sin(jnp.pi * jnp.full((short, long), number_ref[0], F32) * freq * freq / width)
    squares = factor * factor
    for ref in term_refs[1:]:
        total += ref[:blk].astype(F32)
        parts = ref[blk:, :long].astype(F32)
        number = (parts[0:1] + parts[1:2]) + parts[2:3]
        factor = jnp.sin(jnp.pi * jnp.broadcast_to(number, (short, long)) * freq * freq / width)
        squares += factor * factor
    sum_ref[...] = total
    matrix = circulant(4.0 * squares - 2.0 * len(term_refs))
    table_ref[:, :width] = matrix
    table_ref[:, width:] = matrix[:, :quarter]


def table_of(number, terms):
    n_dist = len(terms)
    blk, quarter = terms[0].shape
    width = n_dist * quarter
    return pl.pallas_call(
        table_kernel,
        out_shape=(
            jax.ShapeDtypeStruct((DEEP, width + quarter), BF16),
            jax.ShapeDtypeStruct((blk, quarter), F32),
        ),
        in_specs=[whole(pltpu.SMEM)] + [whole()] * n_dist,
        out_specs=[whole()] * 2,
        compiler_params=room(12 * MIB),
        cost_estimate=cost(2**24, 3 * MIB),
        name="table",
    )(number, *terms)


def filter_kernel(n_dist, first, me_ref, own_ref, term_ref, table_ref, *refs):
    parts, out_ref = refs[:n_dist], refs[-1]
    rows, quarter = own_ref.shape
    width = n_dist * quarter
    me = me_ref[0]
    total = (2.0 * n_dist) * own_ref[...] + term_ref[first : first + rows]
    for k, ref in enumerate(parts):
        for h in range(quarter // DEEP):
            start = (me - (me ^ k)) * quarter - h * DEEP + width
            start = pl.multiple_of(lax.rem(start, width), 128)
            total += jnp.dot(
                ref[:, h * DEEP : (h + 1) * DEEP],
                table_ref[:, pl.ds(start, quarter)],
                preferred_element_type=F32,
            )
    out_ref[...] = total.astype(BF16)


def filtered(me, own, term, table, parts, first):
    rows, quarter = own.shape
    n_dist = len(parts)
    return pl.pallas_call(
        functools.partial(filter_kernel, n_dist, first),
        out_shape=jax.ShapeDtypeStruct((rows, quarter), BF16),
        in_specs=[whole(pltpu.SMEM)] + [whole()] * (3 + n_dist),
        out_specs=whole(),
        compiler_params=room(4 * MIB),
        cost_estimate=cost(2 * rows * quarter * quarter * n_dist, 3 * MIB),
        name="filter",
    )(me, own, term, table, *parts)


def back_kernel(owners, me_ref, targets_ref, kernels_ref, *refs):
    parts, (out_hbm, chosen, out, sems) = refs[:-4], refs[-4:]
    vblocks, blk, _ = out.shape
    top = kernels_ref.shape[1]
    for c, (start, rows) in enumerate(chunks_of(blk)):
        for k in range(owners):
            chosen[k, start : start + rows] = parts[c * owners + k][...]
    me = me_ref[0]
    group = 4
    copies = []
    for step in range(vblocks // group):
        for b in range(step * group, (step + 1) * group):
            picked = [chosen[targets_ref[t, b] ^ me] for t in range(top)]
            out[b] = lax.dot_general(
                kernels_ref[b].reshape(top * blk, blk),
                jnp.concatenate(picked, axis=0),
                (((0,), (0,)), ((), ())),
                preferred_element_type=F32,
            ).astype(BF16)
        part = pl.ds(step * group, group)
        copies.append(pltpu.make_async_copy(out.at[part], out_hbm.at[part], sems.at[step]))
        copies[-1].start()
    for copy in copies:
        copy.wait()


def back(me, targets, kernels, parts, owners):
    vblocks, top, blk, _ = kernels.shape
    quarter = parts[0].shape[1]
    return pl.pallas_call(
        functools.partial(back_kernel, owners),
        out_shape=jax.ShapeDtypeStruct((vblocks, blk, quarter), BF16),
        in_specs=[whole(pltpu.SMEM)] * 2 + [whole()] * (1 + len(parts)),
        out_specs=whole(pltpu.HBM),
        scratch_shapes=[
            pltpu.VMEM((owners, blk, quarter), BF16),
            pltpu.VMEM((vblocks, blk, quarter), BF16),
            pltpu.SemaphoreType.DMA((vblocks,)),
        ],
        compiler_params=room(2 * (owners + vblocks) * blk * quarter + 6 * MIB),
        cost_estimate=cost(2 * vblocks * top * blk * blk * quarter, 4 * MIB),
        name="back",
    )(me, targets, kernels, *parts)


def shards(volume, kernels, targets, contrast, fresnel_numbers):
    owners, n_dist = lax.axis_size("rows"), lax.axis_size("dist")
    me_rows = lax.axis_index("rows").astype(jnp.int32).reshape(1)
    me_dist = lax.axis_index("dist").astype(jnp.int32).reshape(1)
    targets = targets.T

    send, keep = project(me_rows, targets, kernels, volume, owners)
    contrast_table = circ(fresnel_numbers, contrast.shape[-1])
    came = swap(send, "rows", 1)
    own, *outgoing = pair_sum(keep, came, 1)
    arrived = []
    for k, x in enumerate(outgoing):
        arrived.append(swap(x, "rows", 2 * (k + 1)))

    terms = terms_of(fresnel_numbers, me_dist, contrast[0, 0], contrast_table, n_dist)
    came = [terms[0]]
    for k in range(1, n_dist):
        came.append(swap(terms[k], "dist", k))
    table, term = table_of(fresnel_numbers, came)

    totals, rounded = total_sum(own, arrived)
    pieces = []
    for c, (start, _) in enumerate(chunks_of(own.shape[0])):
        total = totals[c]
        parts = [rounded[c]]
        for k in range(1, n_dist):
            parts.append(swap(rounded[c], "dist", k))
        image = filtered(me_dist, total, term, table, parts, start)
        found = [image]
        for rel in range(1, owners):
            low = rel & -rel
            found.append(swap(found[rel ^ low], "rows", low))
        pieces += found
    return back(me_rows, targets, kernels, pieces, owners)


def solution(mesh):
    in_specs = (
        P("rows", None, "dist"),
        P("rows", None, None, None),
        P("rows", None),
        P("dist", "rows", None, None),
        P("dist"),
    )
    out_specs = P("rows", None, "dist")

    return jax.shard_map(shards, mesh=mesh, in_specs=in_specs, out_specs=out_specs, check_vma=False)
```

```python
import functools
import math

import jax
import jax.numpy as jnp
from jax import lax
from jax.experimental import pallas as pl
from jax.experimental.pallas import tpu as pltpu
from jax.sharding import PartitionSpec as P


BF16 = jnp.bfloat16
F32 = jnp.float32
DEEP = 256
LANES = 128
SPLIT = (1,)
TREE = False
MIB = 2**20


def whole(memory_space=pltpu.VMEM):
    return pl.BlockSpec(memory_space=memory_space)


def swap(x, axis, mask):
    size = lax.axis_size(axis)
    return lax.ppermute(x, axis, [(i, i ^ mask) for i in range(size)])


def chunks_of(blk):
    unit = blk // sum(SPLIT)
    starts = [unit * sum(SPLIT[:i]) for i in range(len(SPLIT))]
    return [(start, unit * size) for start, size in zip(starts, SPLIT)]


def cost(flops, nbytes):
    return pl.CostEstimate(flops=flops, bytes_accessed=nbytes, transcendentals=0)


def room(nbytes):
    return pltpu.CompilerParams(vmem_limit_bytes=int(nbytes) + 4 * MIB)


def project_kernel(me_ref, *refs):
    targets_hbm, kernels_hbm, volume_hbm, send_far, send_near, keep_far, keep_near = refs[:7]
    targets, kernels, volume, acc, sems, target_sem = refs[7:]
    vblocks, top, blk, _ = kernels.shape
    near, half = send_near.shape[0], acc.shape[0] // 2
    group = 4
    steps = vblocks // group

    def copies(step):
        part = pl.ds(step * group, group)
        return (
            pltpu.make_async_copy(volume_hbm.at[part], volume.at[part], sems.at[0, step]),
            pltpu.make_async_copy(kernels_hbm.at[part], kernels.at[part], sems.at[1, step]),
        )

    get_targets = pltpu.make_async_copy(targets_hbm, targets, target_sem)
    get_targets.start()
    for step in range(steps):
        for copy in copies(step):
            copy.start()
    acc[...] = jnp.zeros_like(acc)
    get_targets.wait()
    me = me_ref[0]

    def body(step, carry):
        for copy in copies(step):
            copy.wait()
        for i in range(group):
            b = step * group + i
            product = jnp.dot(
                kernels[b].reshape(top * blk, blk), volume[b], preferred_element_type=F32
            )
            product = product.astype(BF16).astype(F32)
            for t in range(top):
                rel = targets[t, b] ^ me
                slot = (rel & 1) * half + (rel >> 1)
                acc[slot] += product[t * blk : (t + 1) * blk]
        return carry

    lax.fori_loop(0, steps, body, 0)
    send_far[...] = acc[half + near :].astype(BF16)
    send_near[...] = acc[half : half + near].astype(BF16)
    keep_far[...] = acc[near:half].astype(BF16)
    keep_near[...] = acc[:near].astype(BF16)


def project(me, targets, kernels, volume, owners):
    vblocks, blk, quarter = volume.shape
    top = kernels.shape[1]
    half = owners // 2
    near = half // 2
    parts = [jax.ShapeDtypeStruct((n, blk, quarter), BF16) for n in (half - near, near)]
    inputs = (targets, kernels, volume)
    return pl.pallas_call(
        project_kernel,
        out_shape=parts + parts,
        in_specs=[whole(pltpu.SMEM)] + [whole(pltpu.HBM)] * 3,
        out_specs=[whole()] * 4,
        scratch_shapes=[
            pltpu.SMEM(targets.shape, jnp.int32),
            pltpu.VMEM(kernels.shape, BF16),
            pltpu.VMEM(volume.shape, BF16),
            pltpu.VMEM((owners, blk, quarter), F32),
            pltpu.SemaphoreType.DMA((2, vblocks)),
            pltpu.SemaphoreType.DMA,
        ],
        compiler_params=room(8 * owners * blk * quarter + 8 * MIB),
        cost_estimate=cost(2 * vblocks * top * blk * blk * quarter, 4 * MIB),
        name="project",
    )(me, *(pltpu.with_memory_space_constraint(x, pltpu.HBM) for x in inputs))


def pair_kernel(keep_ref, came_ref, *out_refs):
    for k, ref in enumerate(out_refs):
        ref[...] = (keep_ref[k].astype(F32) + came_ref[k].astype(F32)).astype(ref.dtype)


def pair_sum(keep, came, dtypes):
    n, blk, quarter = keep.shape
    return pl.pallas_call(
        pair_kernel,
        out_shape=[jax.ShapeDtypeStruct((blk, quarter), dtype) for dtype in dtypes],
        in_specs=[whole()] * 2,
        out_specs=[whole()] * n,
        compiler_params=room(8 * n * blk * quarter),
        cost_estimate=cost(n * blk * quarter, 6 * n * blk * quarter),
        name="pair_sum",
    )(keep, came)


def total_kernel(own_ref, *refs):
    total_ref, rounded_ref = refs[-2:]
    total = own_ref[...]
    for ref in refs[:-2]:
        total += ref[...].astype(F32)
    total_ref[...] = total
    rounded_ref[...] = total.astype(BF16)


def total_sum(own, came):
    return pl.pallas_call(
        total_kernel,
        out_shape=[jax.ShapeDtypeStruct(own.shape, d) for d in (F32, BF16)],
        in_specs=[whole()] * (1 + len(came)),
        out_specs=[whole()] * 2,
        compiler_params=room((10 + 2 * len(came)) * own.size),
        cost_estimate=cost(own.size * len(came), 8 * own.size),
        name="total_sum",
    )(own, *came)


def mm(a, b):
    return jnp.dot(a, b, precision=lax.Precision.HIGHEST, preferred_element_type=F32)


def turns(shape, period):
    a = lax.broadcasted_iota(jnp.int32, shape, 0)
    b = lax.broadcasted_iota(jnp.int32, shape, 1)
    angle = (a * b % period).astype(F32) * (2.0 * math.pi / period)
    return jnp.cos(angle), jnp.sin(angle)


def frequencies(short, long):
    k1 = lax.broadcasted_iota(jnp.int32, (short, long), 0)
    k2 = lax.broadcasted_iota(jnp.int32, (short, long), 1)
    freq = k1 + short * k2
    return jnp.minimum(freq, short * long - freq).astype(F32)


def circulant(spec):
    short, long = spec.shape
    width = short * long
    long_c, long_s = turns((long, long), long)
    twist_c, twist_s = turns((short, long), width)
    short_c, short_s = turns((short, short), short)
    yc, ys = mm(spec, long_c), mm(spec, long_s)
    re = yc * twist_c - ys * twist_s
    im = yc * twist_s + ys * twist_c
    g = (mm(short_c, re) - mm(short_s, im)) * (1.0 / width)
    line = jnp.concatenate([g[i : i + 1] for i in range(short)], axis=1)
    spread = jnp.broadcast_to(line, (LANES, width))
    return pltpu.roll(spread, 0, 1, stride=1, stride_axis=0).astype(BF16)


def store_table(table_ref, matrix):
    width, total = matrix.shape[1], table_ref.shape[1]
    for top in range(0, DEEP, LANES):
        rows = slice(top, top + LANES)
        if top:
            table_ref[rows, :top] = matrix[:, width - top :]
        for start in range(top, total, width):
            size = min(width, total - start)
            table_ref[rows, start : start + size] = matrix[:, :size]


def contrast_factor(number, width):
    short, long = width // LANES, LANES
    freq = frequencies(short, long)
    return 2.0 * jnp.sin(jnp.pi * jnp.full((short, long), number, F32) * freq * freq / width)


def circ_kernel(number_ref, spread_ref, table_ref):
    width = table_ref.shape[1] // 2
    spread_ref[...] = jnp.full(spread_ref.shape, number_ref[0], F32)
    store_table(table_ref, circulant(contrast_factor(number_ref[0], width)))


def circ(number, width):
    return pl.pallas_call(
        circ_kernel,
        out_shape=(
            jax.ShapeDtypeStruct((8, LANES), F32),
            jax.ShapeDtypeStruct((DEEP, 2 * width), BF16),
        ),
        in_specs=[whole(pltpu.SMEM)],
        out_specs=[whole()] * 2,
        compiler_params=room(8 * MIB),
        cost_estimate=cost(2**24, 3 * MIB),
        name="circ",
    )(number)


def term_kernel(number_ref, me_ref, contrast_ref, table_ref, *out_refs):
    n_dist = len(out_refs)
    blk, width = contrast_ref.shape
    quarter = width // n_dist
    me = me_ref[0]
    value = jnp.broadcast_to(number_ref[:1, :1], (16, quarter))
    for k, ref in enumerate(out_refs):
        at = (me ^ k) * quarter
        total = jnp.zeros((blk, quarter), F32)
        for i in range(width // DEEP):
            start = pl.multiple_of(lax.rem(width - i * DEEP + at, width), 128)
            total += jnp.dot(
                contrast_ref[:, i * DEEP : (i + 1) * DEEP],
                table_ref[:, pl.ds(start, quarter)],
                preferred_element_type=F32,
            )
        ref[:blk] = total.astype(BF16)
        if k:
            rest, parts = value, []
            for _ in range(3):
                parts.append(rest.astype(BF16).astype(F32))
                rest = rest - parts[-1]
            which = lax.broadcasted_iota(jnp.int32, value.shape, 0)
            packed = jnp.where(which == 0, parts[0], jnp.where(which == 1, parts[1], parts[2]))
            ref[blk:] = packed.astype(BF16)


def terms_of(number, me, contrast, table, n_dist):
    blk, width = contrast.shape
    quarter = width // n_dist
    return pl.pallas_call(
        term_kernel,
        out_shape=[
            jax.ShapeDtypeStruct((blk + (16 if k else 0), quarter), BF16) for k in range(n_dist)
        ],
        in_specs=[whole(), whole(pltpu.SMEM), whole(), whole()],
        out_specs=[whole()] * n_dist,
        compiler_params=room(12 * MIB),
        cost_estimate=cost(2 * blk * width * width, 3 * MIB),
        name="terms",
    )(number, me, contrast, table)


def table_kernel(number_ref, *refs):
    term_refs, (table_ref, sum_ref) = refs[:-2], refs[-2:]
    blk, quarter = sum_ref.shape
    width = table_ref.shape[1] - quarter
    short, long = width // LANES, LANES
    freq = frequencies(short, long)
    total = term_refs[0][...].astype(F32)
    number = jnp.broadcast_to(number_ref[:1], (short, long))
    factor = jnp.sin(jnp.pi * number * freq * freq / width)
    squares = factor * factor
    for ref in term_refs[1:]:
        total += ref[:blk].astype(F32)
        parts = ref[blk:, :long].astype(F32)
        number = (parts[0:1] + parts[1:2]) + parts[2:3]
        factor = jnp.sin(jnp.pi * jnp.broadcast_to(number, (short, long)) * freq * freq / width)
        squares += factor * factor
    sum_ref[...] = total
    matrix = circulant(4.0 * squares - 2.0 * len(term_refs))
    store_table(table_ref, matrix)


def table_of(number, terms):
    n_dist = len(terms)
    blk, quarter = terms[0].shape
    width = n_dist * quarter
    return pl.pallas_call(
        table_kernel,
        out_shape=(
            jax.ShapeDtypeStruct((DEEP, width + quarter), BF16),
            jax.ShapeDtypeStruct((blk, quarter), F32),
        ),
        in_specs=[whole()] * (1 + n_dist),
        out_specs=[whole()] * 2,
        compiler_params=room(12 * MIB),
        cost_estimate=cost(2**24, 3 * MIB),
        name="table",
    )(number, *terms)


def filter_kernel(n_dist, me_ref, own_ref, term_ref, table_ref, *refs):
    parts, out_refs = refs[:n_dist], refs[n_dist:]
    blk, quarter = own_ref.shape
    width = n_dist * quarter
    me = me_ref[0]
    total = (2.0 * n_dist) * own_ref[...] + term_ref[...]
    for k, ref in enumerate(parts):
        for h in range(quarter // DEEP):
            start = (me - (me ^ k)) * quarter - h * DEEP + width
            start = pl.multiple_of(lax.rem(start, width), LANES)
            total += jnp.dot(
                ref[:, h * DEEP : (h + 1) * DEEP],
                table_ref[:, pl.ds(start, quarter)],
                preferred_element_type=F32,
            )
    for ref, (start, rows) in zip(out_refs, chunks_of(blk)):
        ref[...] = total[start : start + rows].astype(BF16)


def filtered(me, own, term, table, parts):
    blk, quarter = own.shape
    n_dist = len(parts)
    outs = [jax.ShapeDtypeStruct((rows, quarter), BF16) for _, rows in chunks_of(blk)]
    return pl.pallas_call(
        functools.partial(filter_kernel, n_dist),
        out_shape=outs,
        in_specs=[whole(pltpu.SMEM)] + [whole()] * (3 + n_dist),
        out_specs=[whole()] * len(outs),
        compiler_params=room(4 * MIB),
        cost_estimate=cost(2 * blk * quarter * quarter * n_dist, 3 * MIB),
        name="filter",
    )(me, own, term, table, *parts)


def back_kernel(owners, me_ref, targets_ref, kernels_ref, *refs):
    parts, (out_hbm, chosen, out, sems) = refs[:-4], refs[-4:]
    vblocks, blk, _ = out.shape
    top = kernels_ref.shape[1]
    for c, (start, rows) in enumerate(chunks_of(blk)):
        for k in range(owners):
            chosen[k, start : start + rows] = parts[c * owners + k][...]
    me = me_ref[0]
    group = 4
    copies = []
    for step in range(vblocks // group):
        for b in range(step * group, (step + 1) * group):
            picked = [chosen[targets_ref[t, b] ^ me] for t in range(top)]
            out[b] = lax.dot_general(
                kernels_ref[b].reshape(top * blk, blk),
                jnp.concatenate(picked, axis=0),
                (((0,), (0,)), ((), ())),
                preferred_element_type=F32,
            ).astype(BF16)
        part = pl.ds(step * group, group)
        copies.append(pltpu.make_async_copy(out.at[part], out_hbm.at[part], sems.at[step]))
        copies[-1].start()
    for copy in copies:
        copy.wait()


def back(me, targets, kernels, parts, owners):
    vblocks, top, blk, _ = kernels.shape
    quarter = parts[0].shape[1]
    return pl.pallas_call(
        functools.partial(back_kernel, owners),
        out_shape=jax.ShapeDtypeStruct((vblocks, blk, quarter), BF16),
        in_specs=[whole(pltpu.SMEM)] * 2 + [whole()] * (1 + len(parts)),
        out_specs=whole(pltpu.HBM),
        scratch_shapes=[
            pltpu.VMEM((owners, blk, quarter), BF16),
            pltpu.VMEM((vblocks, blk, quarter), BF16),
            pltpu.SemaphoreType.DMA((vblocks,)),
        ],
        compiler_params=room(2 * (owners + vblocks) * blk * quarter + 6 * MIB),
        cost_estimate=cost(2 * vblocks * top * blk * blk * quarter, 4 * MIB),
        name="back",
    )(me, targets, kernels, *parts)


def source(rel):
    low = 1 if rel & 1 else (rel & -rel if TREE else rel)
    return rel ^ low, low


def shards(volume, kernels, targets, contrast, fresnel_numbers):
    owners, n_dist = lax.axis_size("rows"), lax.axis_size("dist")
    me_rows = lax.axis_index("rows").astype(jnp.int32).reshape(1)
    me_dist = lax.axis_index("dist").astype(jnp.int32).reshape(1)
    half = owners // 2
    near = half // 2
    targets = targets.T

    send_far, send_near, keep_far, keep_near = project(me_rows, targets, kernels, volume, owners)
    number, contrast_table = circ(fresnel_numbers, contrast.shape[-1])
    came_far = swap(send_far, "rows", 1)
    came_near = swap(send_near, "rows", 1)
    far_sums = pair_sum(keep_far, came_far, [BF16] * (half - near))
    own, *near_sums = pair_sum(keep_near, came_near, [F32] + [BF16] * (near - 1))
    arrived = []
    for k, x in enumerate([*near_sums, *far_sums]):
        arrived.append(swap(x, "rows", 2 * (k + 1)))

    terms = terms_of(number, me_dist, contrast[0, 0], contrast_table, n_dist)
    came = [terms[0]]
    for k in range(1, n_dist):
        came.append(swap(terms[k], "dist", k))
    table, term = table_of(number, came)

    total, rounded = total_sum(own, arrived)
    parts = [rounded]
    for k in range(1, n_dist):
        parts.append(swap(rounded, "dist", k))
    images = filtered(me_dist, total, term, table, parts)
    pieces = []
    for image in images:
        found = [image]
        for rel in range(1, owners):
            origin, mask = source(rel)
            found.append(swap(found[origin], "rows", mask))
        pieces += found
    return back(me_rows, targets, kernels, pieces, owners)


def solution(mesh):
    in_specs = (
        P("rows", None, "dist"),
        P("rows", None, None, None),
        P("rows", None),
        P("dist", "rows", None, None),
        P("dist"),
    )
    out_specs = P("rows", None, "dist")

    return jax.shard_map(shards, mesh=mesh, in_specs=in_specs, out_specs=out_specs, check_vma=False)
```

```python
import functools
import math

import jax
import jax.numpy as jnp
from jax import lax
from jax.experimental import pallas as pl
from jax.experimental.pallas import tpu as pltpu
from jax.sharding import PartitionSpec as P


BF16 = jnp.bfloat16
F32 = jnp.float32
DEEP = 256
LANES = 128
SPLIT = (1,)
TREE = False
MIB = 2**20


def whole(memory_space=pltpu.VMEM):
    return pl.BlockSpec(memory_space=memory_space)


def swap(x, axis, mask):
    size = lax.axis_size(axis)
    return lax.ppermute(x, axis, [(i, i ^ mask) for i in range(size)])


def chunks_of(blk):
    unit = blk // sum(SPLIT)
    starts = [unit * sum(SPLIT[:i]) for i in range(len(SPLIT))]
    return [(start, unit * size) for start, size in zip(starts, SPLIT)]


def cost(flops, nbytes):
    return pl.CostEstimate(flops=flops, bytes_accessed=nbytes, transcendentals=0)


def room(nbytes):
    return pltpu.CompilerParams(vmem_limit_bytes=int(nbytes) + 4 * MIB)


def project_kernel(me_ref, *refs):
    targets_hbm, kernels_hbm, volume_hbm, send_far, send_near, keep_far, keep_near = refs[:7]
    targets, kernels, volume, acc, sems, target_sem = refs[7:]
    vblocks, top, blk, _ = kernels.shape
    near, half = send_near.shape[0], acc.shape[0] // 2
    group = 8
    steps = vblocks // group

    def copies(step):
        part = pl.ds(step * group, group)
        return (
            pltpu.make_async_copy(volume_hbm.at[part], volume.at[part], sems.at[0, step]),
            pltpu.make_async_copy(kernels_hbm.at[part], kernels.at[part], sems.at[1, step]),
        )

    get_targets = pltpu.make_async_copy(targets_hbm, targets, target_sem)
    get_targets.start()
    for step in range(steps):
        for copy in copies(step):
            copy.start()
    acc[...] = jnp.zeros_like(acc)
    get_targets.wait()
    me = me_ref[0]

    for step in range(steps):
        for copy in copies(step):
            copy.wait()
        for i in range(group):
            b = step * group + i
            product = jnp.dot(
                kernels[b].reshape(top * blk, blk), volume[b], preferred_element_type=F32
            )
            product = product.astype(BF16).astype(F32)
            for t in range(top):
                rel = targets[t, b] ^ me
                slot = (rel & 1) * half + (rel >> 1)
                acc[slot] += product[t * blk : (t + 1) * blk]
    send_far[...] = acc[half + near :].astype(BF16)
    send_near[...] = acc[half : half + near].astype(BF16)
    keep_far[...] = acc[near:half].astype(BF16)
    keep_near[...] = acc[:near].astype(BF16)


def project(me, targets, kernels, volume, owners):
    vblocks, blk, quarter = volume.shape
    top = kernels.shape[1]
    half = owners // 2
    near = half // 2
    parts = [jax.ShapeDtypeStruct((n, blk, quarter), BF16) for n in (half - near, near)]
    inputs = (targets, kernels, volume)
    return pl.pallas_call(
        project_kernel,
        out_shape=parts + parts,
        in_specs=[whole(pltpu.SMEM)] + [whole(pltpu.HBM)] * 3,
        out_specs=[whole()] * 4,
        scratch_shapes=[
            pltpu.SMEM(targets.shape, jnp.int32),
            pltpu.VMEM(kernels.shape, BF16),
            pltpu.VMEM(volume.shape, BF16),
            pltpu.VMEM((owners, blk, quarter), F32),
            pltpu.SemaphoreType.DMA((2, vblocks)),
            pltpu.SemaphoreType.DMA,
        ],
        compiler_params=room(8 * owners * blk * quarter + 8 * MIB),
        cost_estimate=cost(2 * vblocks * top * blk * blk * quarter, 4 * MIB),
        name="project",
    )(me, *(pltpu.with_memory_space_constraint(x, pltpu.HBM) for x in inputs))


def pair_kernel(keep_ref, came_ref, *out_refs):
    for k, ref in enumerate(out_refs):
        ref[...] = (keep_ref[k].astype(F32) + came_ref[k].astype(F32)).astype(ref.dtype)


def pair_sum(keep, came, dtypes):
    n, blk, quarter = keep.shape
    return pl.pallas_call(
        pair_kernel,
        out_shape=[jax.ShapeDtypeStruct((blk, quarter), dtype) for dtype in dtypes],
        in_specs=[whole()] * 2,
        out_specs=[whole()] * n,
        compiler_params=room(8 * n * blk * quarter),
        cost_estimate=cost(n * blk * quarter, 6 * n * blk * quarter),
        name="pair_sum",
    )(keep, came)


def total_kernel(own_ref, *refs):
    total_ref, rounded_ref = refs[-2:]
    total = own_ref[...]
    for ref in refs[:-2]:
        total += ref[...].astype(F32)
    total_ref[...] = total
    rounded_ref[...] = total.astype(BF16)


def total_sum(own, came):
    return pl.pallas_call(
        total_kernel,
        out_shape=[jax.ShapeDtypeStruct(own.shape, d) for d in (F32, BF16)],
        in_specs=[whole()] * (1 + len(came)),
        out_specs=[whole()] * 2,
        compiler_params=room((10 + 2 * len(came)) * own.size),
        cost_estimate=cost(own.size * len(came), 8 * own.size),
        name="total_sum",
    )(own, *came)


def mm(a, b):
    return jnp.dot(a, b, precision=lax.Precision.HIGHEST, preferred_element_type=F32)


def turns(shape, period):
    a = lax.broadcasted_iota(jnp.int32, shape, 0)
    b = lax.broadcasted_iota(jnp.int32, shape, 1)
    angle = (a * b % period).astype(F32) * (2.0 * math.pi / period)
    return jnp.cos(angle), jnp.sin(angle)


def frequencies(short, long):
    k1 = lax.broadcasted_iota(jnp.int32, (short, long), 0)
    k2 = lax.broadcasted_iota(jnp.int32, (short, long), 1)
    freq = k1 + short * k2
    return jnp.minimum(freq, short * long - freq).astype(F32)


def circulant(spec):
    short, long = spec.shape
    width = short * long
    long_c, long_s = turns((long, long), long)
    twist_c, twist_s = turns((short, long), width)
    short_c, short_s = turns((short, short), short)
    yc, ys = mm(spec, long_c), mm(spec, long_s)
    re = yc * twist_c - ys * twist_s
    im = yc * twist_s + ys * twist_c
    g = (mm(short_c, re) - mm(short_s, im)) * (1.0 / width)
    line = jnp.concatenate([g[i : i + 1] for i in range(short)], axis=1)
    spread = jnp.broadcast_to(line, (LANES, width))
    return pltpu.roll(spread, 0, 1, stride=1, stride_axis=0).astype(BF16)


def store_table(table_ref, matrix):
    width, total = matrix.shape[1], table_ref.shape[1]
    for top in range(0, DEEP, LANES):
        rows = slice(top, top + LANES)
        if top:
            table_ref[rows, :top] = matrix[:, width - top :]
        for start in range(top, total, width):
            size = min(width, total - start)
            table_ref[rows, start : start + size] = matrix[:, :size]


def contrast_factor(number, width):
    short, long = width // LANES, LANES
    freq = frequencies(short, long)
    return 2.0 * jnp.sin(jnp.pi * jnp.full((short, long), number, F32) * freq * freq / width)


def circ_kernel(number_ref, spread_ref, table_ref):
    width = table_ref.shape[1] // 2
    spread_ref[...] = jnp.full(spread_ref.shape, number_ref[0], F32)
    store_table(table_ref, circulant(contrast_factor(number_ref[0], width)))


def circ(number, width):
    return pl.pallas_call(
        circ_kernel,
        out_shape=(
            jax.ShapeDtypeStruct((8, LANES), F32),
            jax.ShapeDtypeStruct((DEEP, 2 * width), BF16),
        ),
        in_specs=[whole(pltpu.SMEM)],
        out_specs=[whole()] * 2,
        compiler_params=room(8 * MIB),
        cost_estimate=cost(2**24, 3 * MIB),
        name="circ",
    )(number)


def term_kernel(number_ref, me_ref, contrast_ref, table_ref, *out_refs):
    n_dist = len(out_refs)
    blk, width = contrast_ref.shape
    quarter = width // n_dist
    me = me_ref[0]
    value = jnp.broadcast_to(number_ref[:1, :1], (16, quarter))
    for k, ref in enumerate(out_refs):
        at = (me ^ k) * quarter
        total = jnp.zeros((blk, quarter), F32)
        for i in range(width // DEEP):
            start = pl.multiple_of(lax.rem(width - i * DEEP + at, width), 128)
            total += jnp.dot(
                contrast_ref[:, i * DEEP : (i + 1) * DEEP],
                table_ref[:, pl.ds(start, quarter)],
                preferred_element_type=F32,
            )
        ref[:blk] = total.astype(BF16)
        if k:
            rest, parts = value, []
            for _ in range(3):
                parts.append(rest.astype(BF16).astype(F32))
                rest = rest - parts[-1]
            which = lax.broadcasted_iota(jnp.int32, value.shape, 0)
            packed = jnp.where(which == 0, parts[0], jnp.where(which == 1, parts[1], parts[2]))
            ref[blk:] = packed.astype(BF16)


def terms_of(number, me, contrast, table, n_dist):
    blk, width = contrast.shape
    quarter = width // n_dist
    return pl.pallas_call(
        term_kernel,
        out_shape=[
            jax.ShapeDtypeStruct((blk + (16 if k else 0), quarter), BF16) for k in range(n_dist)
        ],
        in_specs=[whole(), whole(pltpu.SMEM), whole(), whole()],
        out_specs=[whole()] * n_dist,
        compiler_params=room(12 * MIB),
        cost_estimate=cost(2 * blk * width * width, 3 * MIB),
        name="terms",
    )(number, me, contrast, table)


def table_kernel(number_ref, *refs):
    term_refs, (table_ref, sum_ref) = refs[:-2], refs[-2:]
    blk, quarter = sum_ref.shape
    width = table_ref.shape[1] - quarter
    short, long = width // LANES, LANES
    freq = frequencies(short, long)
    total = term_refs[0][...].astype(F32)
    number = jnp.broadcast_to(number_ref[:1], (short, long))
    factor = jnp.sin(jnp.pi * number * freq * freq / width)
    squares = factor * factor
    for ref in term_refs[1:]:
        total += ref[:blk].astype(F32)
        parts = ref[blk:, :long].astype(F32)
        number = (parts[0:1] + parts[1:2]) + parts[2:3]
        factor = jnp.sin(jnp.pi * jnp.broadcast_to(number, (short, long)) * freq * freq / width)
        squares += factor * factor
    sum_ref[...] = total
    matrix = circulant(4.0 * squares - 2.0 * len(term_refs))
    store_table(table_ref, matrix)


def table_of(number, terms):
    n_dist = len(terms)
    blk, quarter = terms[0].shape
    width = n_dist * quarter
    return pl.pallas_call(
        table_kernel,
        out_shape=(
            jax.ShapeDtypeStruct((DEEP, width + quarter), BF16),
            jax.ShapeDtypeStruct((blk, quarter), F32),
        ),
        in_specs=[whole()] * (1 + n_dist),
        out_specs=[whole()] * 2,
        compiler_params=room(12 * MIB),
        cost_estimate=cost(2**24, 3 * MIB),
        name="table",
    )(number, *terms)


def filter_kernel(n_dist, me_ref, own_ref, term_ref, table_ref, *refs):
    parts, out_refs = refs[:n_dist], refs[n_dist:]
    blk, quarter = own_ref.shape
    width = n_dist * quarter
    me = me_ref[0]
    total = (2.0 * n_dist) * own_ref[...] + term_ref[...]
    for k, ref in enumerate(parts):
        for h in range(quarter // DEEP):
            start = (me - (me ^ k)) * quarter - h * DEEP + width
            start = pl.multiple_of(lax.rem(start, width), LANES)
            total += jnp.dot(
                ref[:, h * DEEP : (h + 1) * DEEP],
                table_ref[:, pl.ds(start, quarter)],
                preferred_element_type=F32,
            )
    for ref, (start, rows) in zip(out_refs, chunks_of(blk)):
        ref[...] = total[start : start + rows].astype(BF16)


def filtered(me, own, term, table, parts):
    blk, quarter = own.shape
    n_dist = len(parts)
    outs = [jax.ShapeDtypeStruct((rows, quarter), BF16) for _, rows in chunks_of(blk)]
    return pl.pallas_call(
        functools.partial(filter_kernel, n_dist),
        out_shape=outs,
        in_specs=[whole(pltpu.SMEM)] + [whole()] * (3 + n_dist),
        out_specs=[whole()] * len(outs),
        compiler_params=room(4 * MIB),
        cost_estimate=cost(2 * blk * quarter * quarter * n_dist, 3 * MIB),
        name="filter",
    )(me, own, term, table, *parts)


def back_kernel(owners, me_ref, targets_ref, kernels_ref, *refs):
    parts, (out_hbm, chosen, out, sems) = refs[:-4], refs[-4:]
    vblocks, blk, _ = out.shape
    top = kernels_ref.shape[1]
    for c, (start, rows) in enumerate(chunks_of(blk)):
        for k in range(owners):
            chosen[k, start : start + rows] = parts[c * owners + k][...]
    me = me_ref[0]
    group = 4
    copies = []
    for step in range(vblocks // group):
        for b in range(step * group, (step + 1) * group):
            picked = [chosen[targets_ref[t, b] ^ me] for t in range(top)]
            out[b] = lax.dot_general(
                kernels_ref[b].reshape(top * blk, blk),
                jnp.concatenate(picked, axis=0),
                (((0,), (0,)), ((), ())),
                preferred_element_type=F32,
            ).astype(BF16)
        part = pl.ds(step * group, group)
        copies.append(pltpu.make_async_copy(out.at[part], out_hbm.at[part], sems.at[step]))
        copies[-1].start()
    for copy in copies:
        copy.wait()


def back(me, targets, kernels, parts, owners):
    vblocks, top, blk, _ = kernels.shape
    quarter = parts[0].shape[1]
    return pl.pallas_call(
        functools.partial(back_kernel, owners),
        out_shape=jax.ShapeDtypeStruct((vblocks, blk, quarter), BF16),
        in_specs=[whole(pltpu.SMEM)] * 2 + [whole()] * (1 + len(parts)),
        out_specs=whole(pltpu.HBM),
        scratch_shapes=[
            pltpu.VMEM((owners, blk, quarter), BF16),
            pltpu.VMEM((vblocks, blk, quarter), BF16),
            pltpu.SemaphoreType.DMA((vblocks,)),
        ],
        compiler_params=room(2 * (owners + vblocks) * blk * quarter + 6 * MIB),
        cost_estimate=cost(2 * vblocks * top * blk * blk * quarter, 4 * MIB),
        name="back",
    )(me, targets, kernels, *parts)


def source(rel):
    low = 1 if rel & 1 else (rel & -rel if TREE else rel)
    return rel ^ low, low


def shards(volume, kernels, targets, contrast, fresnel_numbers):
    owners, n_dist = lax.axis_size("rows"), lax.axis_size("dist")
    me_rows = lax.axis_index("rows").astype(jnp.int32).reshape(1)
    me_dist = lax.axis_index("dist").astype(jnp.int32).reshape(1)
    half = owners // 2
    near = half // 2
    targets = targets.T

    send_far, send_near, keep_far, keep_near = project(me_rows, targets, kernels, volume, owners)
    number, contrast_table = circ(fresnel_numbers, contrast.shape[-1])
    came_far = swap(send_far, "rows", 1)
    came_near = swap(send_near, "rows", 1)
    far_sums = pair_sum(keep_far, came_far, [BF16] * (half - near))
    own, *near_sums = pair_sum(keep_near, came_near, [F32] + [BF16] * (near - 1))
    arrived = []
    for k, x in enumerate([*near_sums, *far_sums]):
        arrived.append(swap(x, "rows", 2 * (k + 1)))

    terms = terms_of(number, me_dist, contrast[0, 0], contrast_table, n_dist)
    came = [terms[0]]
    for k in range(1, n_dist):
        came.append(swap(terms[k], "dist", k))
    table, term = table_of(number, came)

    total, rounded = total_sum(own, arrived)
    parts = [rounded]
    for k in range(1, n_dist):
        parts.append(swap(rounded, "dist", k))
    images = filtered(me_dist, total, term, table, parts)
    pieces = []
    for image in images:
        found = [image]
        for rel in range(1, owners):
            origin, mask = source(rel)
            found.append(swap(found[origin], "rows", mask))
        pieces += found
    return back(me_rows, targets, kernels, pieces, owners)


def solution(mesh):
    in_specs = (
        P("rows", None, "dist"),
        P("rows", None, None, None),
        P("rows", None),
        P("dist", "rows", None, None),
        P("dist"),
    )
    out_specs = P("rows", None, "dist")

    return jax.shard_map(shards, mesh=mesh, in_specs=in_specs, out_specs=out_specs, check_vma=False)
```
